32 devices in a mesh: energy: 2 (over y), slab: 4 (over z), orb: 2 (over x), rhs: 2 (over core).
Axes of the slice: x: 2, y: 2, z: 4, core: 2. Of those that a mesh axis runs over, the one named last changes fastest.
Arguments:
- diag_blocks: float32 [16, 192, 384], P(('energy', 'slab'), 'orb'), parts along dimension 0, may hold values from -8 to 8, as said below
- couplings: float32 [16, 192, 384], P(('energy', 'slab')), parts along dimension 0, may hold values from -8 to 8
- sources: float32 [16, 32, 384], P(('energy', 'slab'), ('orb', 'rhs')), parts along dimension 0, may hold values from -8 to 8
Outputs:
- solution: float32 [16, 32, 384], P(('energy', 'slab'), ('orb', 'rhs')), parts along dimension 0
The draws below stay inside these ranges and needn't reach their ends.
There are 2 independent parts, one for each index of `energy`. The reference program is written for one: setup_inputs(seed, part) draws one part's arguments, and reference() takes and returns one part's arrays. A program takes and returns all parts, laid end to end along the dimension named above; each array names one. Nothing has to cross between parts.
Inputs may be any that keep to these rules, and one draw needn't show every extreme that they name: Every diag_blocks[n] is Hermitian, and together with couplings it makes K positive definite with smallest eigenvalue 0.01 or more.
All inputs are finite; a program needn't handle non-finite values.
Results may differ from the reference program's by a relative error of at most 0.0003.
Values sent between devices are 32-bit elements; how exact they have to be, the bound alone decides.
A program may use at most 128 MiB of HBM per device.

```python
import math
import jax
import jax.numpy as jnp
from jax import lax

NO = 192
NL = 8
NRHS = 32


def layer_matrices(key):
    base = jax.random.fold_in(key, 1723)
    keys = jax.random.split(base, 6)
    spread = 0.5 / math.sqrt(2.0 * NO)
    identity = jnp.eye(NO, dtype=jnp.float32)
    left_real = identity + spread * jax.random.normal(keys[0], (NL, NO, NO), jnp.float32)
    left_imag = spread * jax.random.normal(keys[1], (NL, NO, NO), jnp.float32)
    right_real = identity + spread * jax.random.normal(keys[2], (NL, NO, NO), jnp.float32)
    right_imag = spread * jax.random.normal(keys[3], (NL, NO, NO), jnp.float32)
    level_shift = jnp.exp(jax.random.uniform(keys[4], (), jnp.float32, math.log(0.01), math.log(0.03)))
    shifts = level_shift * jnp.exp(jax.random.uniform(keys[5], (NL,), jnp.float32, 0.0, math.log(4.0)))
    return (left_real, left_imag, right_real, right_imag, shifts)


def hermitian_product(first_real, first_imag, second_real, second_imag):
    real_part = jnp.einsum('nki,nkj->nij', first_real, second_real) + jnp.einsum('nki,nkj->nij', first_imag, second_imag)
    imag_part = jnp.einsum('nki,nkj->nij', first_real, second_imag) - jnp.einsum('nki,nkj->nij', first_imag, second_real)
    return (real_part, imag_part)


def column_major(real_part, imag_part):
    return jnp.concatenate([jnp.swapaxes(real_part, 1, 2), jnp.swapaxes(imag_part, 1, 2)], axis=2)


def draw_diag_blocks(key, part):
    left_real, left_imag, right_real, right_imag, shifts = layer_matrices(key)
    own_real, own_imag = hermitian_product(right_real, right_imag, right_real, right_imag)
    next_real, next_imag = hermitian_product(left_real, left_imag, left_real, left_imag)
    has_above = (jnp.arange(NL) >= 1).astype(jnp.float32)[:, None, None]
    padding = jnp.zeros((1, NO, NO), jnp.float32)
    below_real = jnp.concatenate([next_real[1:], padding], axis=0)
    below_imag = jnp.concatenate([next_imag[1:], padding], axis=0)
    identity = jnp.eye(NO, dtype=jnp.float32)
    real_part = has_above * own_real + below_real + shifts[:, None, None] * identity
    imag_part = has_above * own_imag + below_imag
    return column_major(real_part, imag_part)


def draw_couplings(key, part):
    left_real, left_imag, right_real, right_imag, shifts = layer_matrices(key)
    cross_real, cross_imag = hermitian_product(right_real, right_imag, left_real, left_imag)
    has_above = (jnp.arange(NL) >= 1).astype(jnp.float32)[:, None, None]
    return column_major(-has_above * cross_real, -has_above * cross_imag)


def draw_sources(key, part):
    base = jax.random.fold_in(key, 3301)
    keys = jax.random.split(base, 1)
    return jnp.clip(jax.random.normal(keys[0], (NL, NRHS, 2 * NO), jnp.float32), -6.0, 6.0)


def setup_inputs(seed: int = 0, part: int = 0) -> dict:
    seeds = jax.random.split(jax.random.key(seed), 4)
    own_keys = jax.random.split(jax.random.fold_in(seeds[3], part), 4)
    return {
        "diag_blocks": draw_diag_blocks(jax.random.fold_in(jax.random.fold_in(seeds[3], part), 71), part),
        "couplings": draw_couplings(jax.random.fold_in(jax.random.fold_in(seeds[3], part), 71), part),
        "sources": draw_sources(jax.random.fold_in(jax.random.fold_in(seeds[3], part), 71), part),
    }


def embed(columns):
    block_order = columns.shape[-1] // 2
    turned = jnp.concatenate([-columns[..., block_order:], columns[..., :block_order]], axis=-1)
    return jnp.concatenate([columns, turned], axis=-2)

def times(left, right):
    return jnp.dot(left.astype(jnp.float32), right.astype(jnp.float32), precision=lax.Precision.HIGHEST, preferred_element_type=jnp.float32)

def times_flipped(left, right):
    return lax.dot_general(left.astype(jnp.float32), right.astype(jnp.float32), (((1,), (1,)), ((), ())), precision=lax.Precision.HIGHEST, preferred_element_type=jnp.float32)

def apply_inverse(factor, rows):
    return jax.scipy.linalg.cho_solve((factor, True), rows.T).T

def reference(diag_blocks, couplings, sources):
    layer_count = diag_blocks.shape[0]
    block_order = diag_blocks.shape[2] // 2
    keep = (jnp.arange(layer_count) > 0).astype(couplings.dtype)
    couplings = couplings * keep[:, None, None]
    embedded = jax.vmap(embed)(couplings)

    def forward(carry, item):
        factor_prev, load_prev = carry
        block, coupling_embed, source = item
        herm_block = coupling_embed[:, :block_order].T
        pivot = block - times(apply_inverse(factor_prev, herm_block), coupling_embed)
        load = source - times(apply_inverse(factor_prev, load_prev), coupling_embed)
        factor = jnp.linalg.cholesky(embed(pivot))
        return ((factor, load), (factor, load))
    start_factor = jnp.eye(2 * block_order, dtype=diag_blocks.dtype)
    start_load = jnp.zeros_like(sources[0])
    _, (factors, loads) = lax.scan(forward, (start_factor, start_load), (diag_blocks, embedded, sources))
    next_embeds = jnp.concatenate([embedded[1:], jnp.zeros_like(embedded[:1])], axis=0)

    def backward(upper_value, item):
        factor, load, next_embed = item
        value = apply_inverse(factor, load - times_flipped(upper_value, next_embed))
        return (value, value)
    _, solution = lax.scan(backward, jnp.zeros_like(sources[0]), (factors, loads, next_embeds), reverse=True)
    return solution
```

```python
import jax
import jax.numpy as jnp
from jax import lax
from jax.sharding import PartitionSpec as P
from jax.experimental import pallas as pl
from jax.experimental.pallas import tpu as pltpu

HALF = 64
LANES = 2 * HALF


def dot(left, right, dims=((1,), (0,))):
    return lax.dot_general(
        left,
        right,
        (dims, ((), ())),
        precision=lax.Precision.HIGHEST,
        preferred_element_type=jnp.float32,
    )


def dot_flipped(left, right):
    return dot(left, right, ((1,), (1,)))


def lane_sign(shape):
    lane = lax.broadcasted_iota(jnp.int32, shape, 1)
    return jnp.where(lane % LANES < HALF, -1.0, 1.0).astype(jnp.float32)


def times_i(rows):
    pieces = [
        pltpu.roll(rows[:, start : start + LANES], HALF, 1)
        for start in range(0, rows.shape[1], LANES)
    ]
    turned = pieces[0] if len(pieces) == 1 else jnp.concatenate(pieces, axis=1)
    return turned * lane_sign(turned.shape)


def interleave(rows):
    count = rows.shape[1] // LANES
    pieces = []
    for chunk in range(count):
        pieces.append(rows[:, chunk * HALF : (chunk + 1) * HALF])
        pieces.append(rows[:, (count + chunk) * HALF : (count + chunk + 1) * HALF])
    return jnp.concatenate(pieces, axis=1)


def separate(rows):
    count = rows.shape[1] // LANES
    pieces = [rows[:, 2 * chunk * HALF : (2 * chunk + 1) * HALF] for chunk in range(count)]
    pieces += [rows[:, (2 * chunk + 1) * HALF : (2 * chunk + 2) * HALF] for chunk in range(count)]
    return jnp.concatenate(pieces, axis=1)


def embed(rows):
    turned = times_i(rows)
    pieces = []
    for start in range(0, rows.shape[0], HALF):
        pieces += [rows[start : start + HALF], turned[start : start + HALF]]
    return jnp.concatenate(pieces, axis=0)


def compact(embedded):
    return jnp.concatenate(
        [embedded[start : start + HALF] for start in range(0, embedded.shape[0], LANES)], axis=0
    )


GROUP = 8


def invert_group(rows, first, sign, lane, row_id):
    for offset in range(0, GROUP, 2):
        step = first + offset
        at_zero = lane == step
        at_one = lane == step + 1
        at_any = at_zero | at_one | (lane == step + HALF) | (lane == step + 1 + HALF)
        zero_real, zero_imag, one_real, one_imag = (
            jnp.broadcast_to(rows[:, at : at + 1], (GROUP, LANES))
            for at in (step, step + HALF, step + 1, step + 1 + HALF)
        )
        head = zero_real[offset : offset + 1]
        tail = one_real[offset + 1 : offset + 2]
        cross_real = one_real[offset : offset + 1]
        cross_imag = one_imag[offset : offset + 1]
        scale = 1.0 / (head * tail - cross_real * cross_real - cross_imag * cross_imag)
        cleared = jnp.where(at_any, 0.0, rows)
        turned = pltpu.roll(cleared, HALF, 1) * sign
        row_zero = cleared[offset : offset + 1] + jnp.where(at_zero, 1.0, 0.0)
        row_one = cleared[offset + 1 : offset + 2] + jnp.where(at_one, 1.0, 0.0)
        turn_zero = turned[offset : offset + 1] + jnp.where(lane == step + HALF, 1.0, 0.0)
        turn_one = turned[offset + 1 : offset + 2] + jnp.where(lane == step + 1 + HALF, 1.0, 0.0)
        new_zero = (tail * row_zero - cross_real * row_one - cross_imag * turn_one) * scale
        new_one = (head * row_one - cross_real * row_zero + cross_imag * turn_zero) * scale
        spin_zero = (tail * turn_zero - cross_real * turn_one + cross_imag * row_one) * scale
        spin_one = (head * turn_one - cross_real * turn_zero - cross_imag * row_zero) * scale
        fresh = (
            cleared
            - (zero_real * new_zero + zero_imag * spin_zero)
            - (one_real * new_one + one_imag * spin_one)
        )
        rows = jnp.where(
            row_id == offset, new_zero, jnp.where(row_id == offset + 1, new_one, fresh)
        )
    return rows


def invert_small(block):
    lane = lax.broadcasted_iota(jnp.int32, (1, LANES), 1)
    row_id = lax.broadcasted_iota(jnp.int32, (GROUP, 1), 0)
    sign = lane_sign((1, LANES))
    groups = [block[start : start + GROUP] for start in range(0, HALF, GROUP)]
    for home in range(len(groups)):
        first = home * GROUP
        done = invert_group(groups[home], first, sign, lane, row_id)
        spun = pltpu.roll(done, HALF, 1) * sign
        inside = (lane % HALF >= first) & (lane % HALF < first + GROUP)
        for index, group in enumerate(groups):
            if index == home:
                continue
            fresh = jnp.where(inside, 0.0, group)
            for at in range(GROUP):
                fresh = fresh - (
                    group[:, first + at : first + at + 1] * done[at : at + 1]
                    + group[:, first + at + HALF : first + at + HALF + 1] * spun[at : at + 1]
                )
            groups[index] = fresh
        groups[home] = done
    return jnp.concatenate(groups, axis=0)


def invert(ref):
    order = ref.shape[0]

    def step(k, carry):
        rows = pl.ds(pl.multiple_of(k * HALF, HALF), HALF)
        lanes = pl.ds(pl.multiple_of(k * LANES, LANES), LANES)
        small = invert_small(ref[rows, lanes])
        panel = ref[rows, :]
        ref[rows, :] = dot(small, jnp.concatenate([panel, times_i(panel)], axis=0))
        ref[rows, lanes] = small
        fresh = ref[rows, :]
        column = ref[:, lanes]
        ref[:, lanes] = jnp.zeros((order, LANES), jnp.float32)
        ref[...] = ref[...] - dot(column, jnp.concatenate([fresh, times_i(fresh)], axis=0))
        ref[rows, :] = fresh
        return carry

    lax.fori_loop(0, order // HALF, step, 0)


def eliminate(pivot_ref, to_pivot_v, to_pivot_u, block_v, block_u, load_i, load_v, load_u):
    order, rhs = block_v.shape[0], load_i.shape[0]
    invert(pivot_ref)
    inverse = embed(pivot_ref[...])
    stacked = [compact(to_pivot_v), load_i]
    if to_pivot_u is not None:
        stacked.append(compact(to_pivot_u))
    through = dot(jnp.concatenate(stacked, axis=0), inverse)
    toward_v = dot_flipped(through[: order + rhs], to_pivot_v)
    new_v = jnp.concatenate([block_v, load_v], axis=0) - toward_v
    kept = (through[:order], through[order : order + rhs])
    if to_pivot_u is None:
        return new_v, kept
    toward_u = dot_flipped(through, to_pivot_u)
    new_u = jnp.concatenate([block_u, load_u], axis=0) - jnp.concatenate(
        [toward_u[order + rhs :], toward_u[order : order + rhs]], axis=0
    )
    return new_v, new_u, -toward_u[:order], kept + (through[order + rhs :],)


def flip_where(flip, ref, embedded):
    @pl.when(flip)
    def _():
        ref[...] = embedded.T

    @pl.when(jnp.logical_not(flip))
    def _():
        ref[...] = embedded


def is_left():
    return lax.axis_index("slab") < lax.axis_size("slab") // 2


def interior_kernel(diag, inner, outer, loads, new_v, new_u, cross, kept_v, kept_b, kept_u, pivot, to_v, to_u):
    left = is_left()
    order = diag.shape[1]
    at_interior = jnp.where(left, 0, 1)
    flip_where(left, to_v, embed(interleave(inner[...])))
    flip_where(jnp.logical_not(left), to_u, embed(interleave(outer[...])))
    pivot[...] = interleave(diag[at_interior])
    load_i = interleave(loads[at_interior])
    load_v = interleave(loads[1 - at_interior])
    block_v = interleave(diag[1 - at_interior])
    zero = jnp.zeros_like(block_v)
    new_v[...], new_u[...], cross[...], kept = eliminate(
        pivot, to_v[...], to_u[...], block_v, zero, load_i, load_v, jnp.zeros_like(load_v)
    )
    kept_v[...], kept_b[...], kept_u[...] = kept


def level_kernel(own_v, own_u, own_cross, first_v, new_v, kept_v, kept_b, pivot):
    order = pivot.shape[0]
    joined = first_v[...] + own_u[...]
    pivot[...] = joined[:order]
    new_v[...], kept = eliminate(
        pivot, embed(own_cross[...]), None, own_v[:order], None, joined[order:], own_v[order:], None
    )
    kept_v[...], kept_b[...] = kept


def wide_level_kernel(
    own_v, own_u, own_cross, first_v, first_u, first_cross,
    new_v, new_u, cross, kept_v, kept_b, kept_u, pivot,
):
    order = pivot.shape[0]
    joined = first_v[...] + own_u[...]
    pivot[...] = joined[:order]
    new_v[...], new_u[...], cross[...], kept = eliminate(
        pivot,
        embed(own_cross[...]),
        embed(first_cross[...]).T,
        own_v[:order],
        first_u[:order],
        joined[order:],
        own_v[order:],
        first_u[order:],
    )
    kept_v[...], kept_b[...], kept_u[...] = kept


def center_kernel(own, other, coupling, value, pivot, to_other):
    order = pivot.shape[0]
    flip_where(jnp.logical_not(is_left()), to_other, embed(interleave(coupling[...])))
    pivot[...] = other[:order]
    reduced, _ = eliminate(
        pivot, to_other[...], None, own[:order], None, other[order:], own[order:], None
    )
    pivot[...] = reduced[:order]
    invert(pivot)
    value[...] = dot(reduced[order:], embed(pivot[...]))


def back_kernel(value_v, value_u, kept_v, kept_b, kept_u, middle):
    middle[...] = (
        kept_b[...]
        - dot(value_v[...], embed(kept_v[...]))
        - dot(value_u[...], embed(kept_u[...]))
    )


def narrow_back_kernel(value_v, kept_v, kept_b, middle):
    middle[...] = kept_b[...] - dot(value_v[...], embed(kept_v[...]))


def final_kernel(value_v, value_u, kept_v, kept_b, kept_u, result):
    middle = (
        kept_b[...]
        - dot(value_v[...], embed(kept_v[...]))
        - dot(value_u[...], embed(kept_u[...]))
    )
    at_interior = jnp.where(is_left(), 0, 1)
    result[at_interior] = separate(middle)
    result[1 - at_interior] = separate(value_v[...])


def call(kernel, outs, scratch, *operands):
    return pl.pallas_call(
        kernel,
        out_shape=[jax.ShapeDtypeStruct(shape, jnp.float32) for shape in outs],
        scratch_shapes=[pltpu.VMEM(shape, jnp.float32) for shape in scratch],
        compiler_params=pltpu.CompilerParams(vmem_limit_bytes=48 * 1024 * 1024),
    )(*operands)


def gather_columns(shard):
    size = lax.axis_size("orb")
    index = lax.axis_index("orb")
    distance = 1
    while distance < size:
        theirs = lax.ppermute(shard, "orb", [(i, i ^ distance) for i in range(size)])
        first = index // distance % 2 == 0
        shard = jnp.where(
            first,
            jnp.concatenate([shard, theirs], axis=1),
            jnp.concatenate([theirs, shard], axis=1),
        )
        distance *= 2
    return shard


def local(diag_blocks, couplings, sources):
    order, width = couplings.shape[1:]
    rhs = sources.shape[1]
    slabs = lax.axis_size("slab")
    half = slabs // 2
    slab = lax.axis_index("slab")
    left = slab < half
    place = jnp.where(left, slab, slabs - 1 - slab)

    def at(position):
        return (position, slabs - 1 - position)

    shifted = lax.ppermute(couplings[0], "slab", [(i, i - 1) for i in range(half, slabs)])
    diag = gather_columns(diag_blocks)
    outer = jnp.where(left, jnp.where(slab > 0, couplings[0], 0.0), shifted)
    center = jnp.where(left, shifted, couplings[0])
    square, tall, thin, full = (order, width), (order + rhs, width), (rhs, width), (width, width)

    new_v, new_u, cross, kept_v, kept_b, kept_u = call(
        interior_kernel,
        [tall, tall, square, square, thin, square],
        [square, full, full],
        diag, couplings[1], outer, sources,
    )
    levels = half.bit_length() - 1
    stored = []
    for level in range(levels):
        distance = 2**level
        firsts = range(distance - 1, half, 2 * distance)
        pairs = [
            (a, b) for first in firsts for a, b in zip(at(first), at(first + distance), strict=True)
        ]
        first_v = lax.ppermute(new_v, "slab", pairs)
        if level == levels - 1:
            new_v, level_v, level_b = call(
                level_kernel, [tall, square, thin], [square], new_v, new_u, cross, first_v
            )
            stored.append((distance, pairs, (level_v, level_b)))
        else:
            first_u = lax.ppermute(new_u, "slab", pairs)
            first_cross = lax.ppermute(cross, "slab", pairs)
            new_v, new_u, cross, level_v, level_b, level_u = call(
                wide_level_kernel,
                [tall, tall, square, square, thin, square],
                [square],
                new_v, new_u, cross, first_v, first_u, first_cross,
            )
            stored.append((distance, pairs, (level_v, level_b, level_u)))
    other = lax.ppermute(new_v, "slab", [(half - 1, half), (half, half - 1)])
    (value_v,) = call(center_kernel, [thin], [square, full], new_v, other, center)
    value_u = jnp.zeros_like(value_v)
    for distance, pairs, kept in reversed(stored):
        if len(kept) == 2:
            (middle,) = call(narrow_back_kernel, [thin], [], value_v, *kept)
        else:
            (middle,) = call(back_kernel, [thin], [], value_v, value_u, *kept)
        sent = lax.ppermute(
            jnp.concatenate([middle, value_u]), "slab", [(b, a) for a, b in pairs]
        )
        is_first = place % (2 * distance) == distance - 1
        value_v = jnp.where(is_first, sent[:rhs], value_v)
        value_u = jnp.where(is_first, sent[rhs:], middle)
    (result,) = call(
        final_kernel, [sources.shape], [], value_v, value_u, kept_v, kept_b, kept_u
    )
    return result


def solution(mesh):
    placed = (
        P(("energy", "slab"), "orb", None),
        P(("energy", "slab"), None, None),
        P(("energy", "slab"), ("orb", "rhs"), None),
    )
    return jax.shard_map(
        local,
        mesh=mesh,
        in_specs=placed,
        out_specs=P(("energy", "slab"), ("orb", "rhs"), None),
        check_vma=False,
    )
```

```python
import jax
import jax.numpy as jnp
from jax import lax
from jax.sharding import PartitionSpec as P
from jax.experimental import pallas as pl
from jax.experimental.pallas import tpu as pltpu

HALF = 64
LANES = 2 * HALF


def dot(left, right, dims=((1,), (0,))):
    return lax.dot_general(
        left,
        right,
        (dims, ((), ())),
        precision=lax.Precision.HIGHEST,
        preferred_element_type=jnp.float32,
    )


def dot_flipped(left, right):
    return dot(left, right, ((1,), (1,)))


def lane_sign(shape):
    lane = lax.broadcasted_iota(jnp.int32, shape, 1)
    return jnp.where(lane % LANES < HALF, -1.0, 1.0).astype(jnp.float32)


def times_i(rows):
    pieces = [
        pltpu.roll(rows[:, start : start + LANES], HALF, 1)
        for start in range(0, rows.shape[1], LANES)
    ]
    turned = pieces[0] if len(pieces) == 1 else jnp.concatenate(pieces, axis=1)
    return turned * lane_sign(turned.shape)


def interleave(rows):
    count = rows.shape[1] // LANES
    pieces = []
    for chunk in range(count):
        pieces.append(rows[:, chunk * HALF : (chunk + 1) * HALF])
        pieces.append(rows[:, (count + chunk) * HALF : (count + chunk + 1) * HALF])
    return jnp.concatenate(pieces, axis=1)


def separate(rows):
    count = rows.shape[1] // LANES
    pieces = [rows[:, 2 * chunk * HALF : (2 * chunk + 1) * HALF] for chunk in range(count)]
    pieces += [rows[:, (2 * chunk + 1) * HALF : (2 * chunk + 2) * HALF] for chunk in range(count)]
    return jnp.concatenate(pieces, axis=1)


def embed(rows):
    turned = times_i(rows)
    pieces = []
    for start in range(0, rows.shape[0], HALF):
        pieces += [rows[start : start + HALF], turned[start : start + HALF]]
    return jnp.concatenate(pieces, axis=0)


def compact(embedded):
    return jnp.concatenate(
        [embedded[start : start + HALF] for start in range(0, embedded.shape[0], LANES)], axis=0
    )


GROUP = 16
TALL = 8


def product(left, right):
    return (left[0] * right[0] - left[1] * right[1], left[0] * right[1] + left[1] * right[0])


def conjugate(value):
    return (value[0], -value[1])


def plus(left, right):
    return (left[0] + right[0], left[1] + right[1])


def minus(left, right):
    return (left[0] - right[0], left[1] - right[1])


def squared(value):
    return value[0] * value[0] + value[1] * value[1]


def scaled_by(value, factor):
    return (value[0] * factor, value[1] * factor)


def invert_pair(head, cross, tail):
    scale = 1.0 / (head * tail - squared(cross))
    return tail * scale, scaled_by(cross, -scale), head * scale


def invert_four(at):
    head = invert_pair(at[0][0][0], at[0][1], at[1][1][0])
    upper = [[at[0][2], at[0][3]], [at[1][2], at[1][3]]]
    mixed = [
        [plus(scaled_by(upper[0][j], head[0]), product(head[1], upper[1][j])) for j in range(2)],
        [
            plus(product(conjugate(head[1]), upper[0][j]), scaled_by(upper[1][j], head[2]))
            for j in range(2)
        ],
    ]

    def schur(i, j):
        return plus(
            product(conjugate(upper[0][i]), mixed[0][j]),
            product(conjugate(upper[1][i]), mixed[1][j]),
        )

    tail = invert_pair(
        at[2][2][0] - schur(0, 0)[0],
        minus(at[2][3], schur(0, 1)),
        at[3][3][0] - schur(1, 1)[0],
    )
    carried = [
        [
            plus(scaled_by(mixed[i][0], tail[0]), product(mixed[i][1], conjugate(tail[1]))),
            plus(product(mixed[i][0], tail[1]), scaled_by(mixed[i][1], tail[2])),
        ]
        for i in range(2)
    ]

    def corner(i, j):
        return plus(
            product(carried[i][0], conjugate(mixed[j][0])),
            product(carried[i][1], conjugate(mixed[j][1])),
        )

    zero = jnp.zeros_like(head[0])
    result = [[None] * 4 for _ in range(4)]
    result[0][0] = (head[0] + corner(0, 0)[0], zero)
    result[0][1] = plus(head[1], corner(0, 1))
    result[1][1] = (head[2] + corner(1, 1)[0], zero)
    result[2][2], result[2][3], result[3][3] = (tail[0], zero), tail[1], (tail[2], zero)
    for i in range(2):
        for j in range(2):
            result[i][2 + j] = (-carried[i][j][0], -carried[i][j][1])
    for i in range(4):
        for j in range(i):
            result[i][j] = conjugate(result[j][i])
    return result


def spread_row(rows, at):
    return jnp.broadcast_to(rows[at : at + 1], (TALL, LANES))


def spread_lane(rows, at):
    return jnp.broadcast_to(rows[:, at : at + 1], (TALL, LANES))


def invert_group(rows, first, sign, lane, row_id):
    parts = [rows[start : start + TALL] for start in range(0, GROUP, TALL)]
    for offset in range(0, GROUP, 4):
        step = first + offset
        home, inner = divmod(offset, TALL)
        columns = [
            [(spread_lane(part, step + at), spread_lane(part, step + at + HALF)) for at in range(4)]
            for part in parts
        ]
        inverse = invert_four(
            [
                [
                    tuple(spread_row(value, inner + i) for value in columns[home][j])
                    if j >= i
                    else None
                    for j in range(4)
                ]
                for i in range(4)
            ]
        )
        inside = (lane % HALF >= step) & (lane % HALF < step + 4)
        cleared = jnp.where(inside, 0.0, parts[home])
        turned = pltpu.roll(cleared, HALF, 1) * sign
        plain, spun = [], []
        for at in range(4):
            plain.append(spread_row(cleared, inner + at) + jnp.where(lane == step + at, 1.0, 0.0))
            spun.append(
                spread_row(turned, inner + at) + jnp.where(lane == step + at + HALF, 1.0, 0.0)
            )
        new_rows, new_spins = [], []
        for i in range(4):
            new = spin = None
            for j in range(4):
                real, imag = inverse[i][j]
                if i == j:
                    term, turn = real * plain[j], real * spun[j]
                else:
                    term = real * plain[j] + imag * spun[j]
                    turn = real * spun[j] - imag * plain[j]
                new, spin = (term, turn) if new is None else (new + term, spin + turn)
            new_rows.append(new)
            new_spins.append(spin)
        updated = []
        for index, part in enumerate(parts):
            fresh = jnp.where(inside, 0.0, part)
            for i in range(4):
                real, imag = columns[index][i]
                fresh = fresh - (real * new_rows[i] + imag * new_spins[i])
            if index == home:
                for i in range(4):
                    fresh = jnp.where(row_id == inner + i, new_rows[i], fresh)
            updated.append(fresh)
        parts = updated
    return jnp.concatenate(parts, axis=0) if len(parts) > 1 else parts[0]


def spread_out(done, spun, first):
    last = HALF - first - GROUP
    before = [jnp.zeros((first, LANES), jnp.float32)] if first else []
    after = [jnp.zeros((last, LANES), jnp.float32)] if last else []
    return jnp.concatenate(before + [done] + after + before + [spun] + after, axis=0)


def invert_small(block):
    lane = lax.broadcasted_iota(jnp.int32, (1, LANES), 1)
    row_id = lax.broadcasted_iota(jnp.int32, (TALL, 1), 0)
    sign = lane_sign((1, LANES))
    group = block[:GROUP]
    for first in range(0, HALF, GROUP):
        done = invert_group(group, first, sign, lane, row_id)
        spun = pltpu.roll(done, HALF, 1) * sign
        inside = (lane % HALF >= first) & (lane % HALF < first + GROUP)
        following = first + GROUP
        if following < HALF:
            old = block[following : following + GROUP]
            group = jnp.where(inside, 0.0, old)
            for at in range(GROUP):
                group = group - (
                    old[:, first + at : first + at + 1] * done[at : at + 1]
                    + old[:, first + at + HALF : first + at + HALF + 1] * spun[at : at + 1]
                )
        rest = jnp.where(inside, 0.0, block) - dot(
            jnp.where(inside, block, 0.0), spread_out(done, spun, first)
        )
        above = [rest[:first]] if first else []
        below = [rest[following:]] if following < HALF else []
        block = jnp.concatenate(above + [done] + below, axis=0)
    return block


def invert(ref):
    order = ref.shape[0]

    def step(k, carry):
        rows = pl.ds(pl.multiple_of(k * HALF, HALF), HALF)
        lanes = pl.ds(pl.multiple_of(k * LANES, LANES), LANES)
        small = invert_small(ref[rows, lanes])
        panel = ref[rows, :]
        ref[rows, :] = dot(small, jnp.concatenate([panel, times_i(panel)], axis=0))
        ref[rows, lanes] = small
        fresh = ref[rows, :]
        column = ref[:, lanes]
        ref[:, lanes] = jnp.zeros((order, LANES), jnp.float32)
        ref[...] = ref[...] - dot(column, jnp.concatenate([fresh, times_i(fresh)], axis=0))
        ref[rows, :] = fresh
        return carry

    lax.fori_loop(0, order // HALF, step, 0)


def eliminate(pivot_ref, to_pivot_v, to_pivot_u, block_v, block_u, load_i, load_v, load_u):
    order, rhs = block_v.shape[0], load_i.shape[0]
    invert(pivot_ref)
    inverse = embed(pivot_ref[...])
    stacked = [compact(to_pivot_v), load_i]
    if to_pivot_u is not None:
        stacked.append(compact(to_pivot_u))
    through = dot(jnp.concatenate(stacked, axis=0), inverse)
    toward_v = dot_flipped(through[: order + rhs], to_pivot_v)
    new_v = jnp.concatenate([block_v, load_v], axis=0) - toward_v
    kept = (through[:order], through[order : order + rhs])
    if to_pivot_u is None:
        return new_v, kept
    toward_u = dot_flipped(through, to_pivot_u)
    new_u = jnp.concatenate([block_u, load_u], axis=0) - jnp.concatenate(
        [toward_u[order + rhs :], toward_u[order : order + rhs]], axis=0
    )
    return new_v, new_u, -toward_u[:order], kept + (through[order + rhs :],)


def flip_where(flip, ref, embedded):
    @pl.when(flip)
    def _():
        ref[...] = embedded.T

    @pl.when(jnp.logical_not(flip))
    def _():
        ref[...] = embedded


def is_left():
    return lax.axis_index("slab") < lax.axis_size("slab") // 2


def interior_kernel(diag, inner, outer, loads, new_v, new_u, cross, kept_v, kept_b, kept_u, pivot, to_v, to_u):
    left = is_left()
    order = diag.shape[1]
    at_interior = jnp.where(left, 0, 1)
    flip_where(left, to_v, embed(interleave(inner[...])))
    flip_where(jnp.logical_not(left), to_u, embed(interleave(outer[...])))
    pivot[...] = interleave(diag[at_interior])
    load_i = interleave(loads[at_interior])
    load_v = interleave(loads[1 - at_interior])
    block_v = interleave(diag[1 - at_interior])
    zero = jnp.zeros_like(block_v)
    new_v[...], new_u[...], cross[...], kept = eliminate(
        pivot, to_v[...], to_u[...], block_v, zero, load_i, load_v, jnp.zeros_like(load_v)
    )
    kept_v[...], kept_b[...], kept_u[...] = kept


def level_kernel(own_v, own_u, own_cross, first_v, new_v, kept_v, kept_b, pivot):
    order = pivot.shape[0]
    joined = first_v[...] + own_u[...]
    pivot[...] = joined[:order]
    new_v[...], kept = eliminate(
        pivot, embed(own_cross[...]), None, own_v[:order], None, joined[order:], own_v[order:], None
    )
    kept_v[...], kept_b[...] = kept


def wide_level_kernel(
    own_v, own_u, own_cross, first_v, first_u, first_cross,
    new_v, new_u, cross, kept_v, kept_b, kept_u, pivot,
):
    order = pivot.shape[0]
    joined = first_v[...] + own_u[...]
    pivot[...] = joined[:order]
    new_v[...], new_u[...], cross[...], kept = eliminate(
        pivot,
        embed(own_cross[...]),
        embed(first_cross[...]).T,
        own_v[:order],
        first_u[:order],
        joined[order:],
        own_v[order:],
        first_u[order:],
    )
    kept_v[...], kept_b[...], kept_u[...] = kept


def center_kernel(own, other, coupling, value, pivot, to_other):
    order = pivot.shape[0]
    flip_where(jnp.logical_not(is_left()), to_other, embed(interleave(coupling[...])))
    pivot[...] = other[:order]
    reduced, _ = eliminate(
        pivot, to_other[...], None, own[:order], None, other[order:], own[order:], None
    )
    pivot[...] = reduced[:order]
    invert(pivot)
    value[...] = dot(reduced[order:], embed(pivot[...]))


def back_kernel(value_v, value_u, kept_v, kept_b, kept_u, middle):
    middle[...] = (
        kept_b[...]
        - dot(value_v[...], embed(kept_v[...]))
        - dot(value_u[...], embed(kept_u[...]))
    )


def narrow_back_kernel(value_v, kept_v, kept_b, middle):
    middle[...] = kept_b[...] - dot(value_v[...], embed(kept_v[...]))


def final_kernel(value_v, value_u, kept_v, kept_b, kept_u, result):
    middle = (
        kept_b[...]
        - dot(value_v[...], embed(kept_v[...]))
        - dot(value_u[...], embed(kept_u[...]))
    )
    at_interior = jnp.where(is_left(), 0, 1)
    result[at_interior] = separate(middle)
    result[1 - at_interior] = separate(value_v[...])


def call(kernel, outs, scratch, *operands):
    return pl.pallas_call(
        kernel,
        out_shape=[jax.ShapeDtypeStruct(shape, jnp.float32) for shape in outs],
        scratch_shapes=[pltpu.VMEM(shape, jnp.float32) for shape in scratch],
        compiler_params=pltpu.CompilerParams(vmem_limit_bytes=48 * 1024 * 1024),
    )(*operands)


def gather_columns(shard):
    size = lax.axis_size("orb")
    index = lax.axis_index("orb")
    distance = 1
    while distance < size:
        theirs = lax.ppermute(shard, "orb", [(i, i ^ distance) for i in range(size)])
        first = index // distance % 2 == 0
        shard = jnp.where(
            first,
            jnp.concatenate([shard, theirs], axis=1),
            jnp.concatenate([theirs, shard], axis=1),
        )
        distance *= 2
    return shard


def local(diag_blocks, couplings, sources):
    order, width = couplings.shape[1:]
    rhs = sources.shape[1]
    slabs = lax.axis_size("slab")
    half = slabs // 2
    slab = lax.axis_index("slab")
    left = slab < half
    place = jnp.where(left, slab, slabs - 1 - slab)

    def at(position):
        return (position, slabs - 1 - position)

    shifted = lax.ppermute(couplings[0], "slab", [(i, i - 1) for i in range(half, slabs)])
    diag = gather_columns(diag_blocks)
    outer = jnp.where(left, jnp.where(slab > 0, couplings[0], 0.0), shifted)
    center = jnp.where(left, shifted, couplings[0])
    square, tall, thin, full = (order, width), (order + rhs, width), (rhs, width), (width, width)

    new_v, new_u, cross, kept_v, kept_b, kept_u = call(
        interior_kernel,
        [tall, tall, square, square, thin, square],
        [square, full, full],
        diag, couplings[1], outer, sources,
    )
    levels = half.bit_length() - 1
    stored = []
    for level in range(levels):
        distance = 2**level
        firsts = range(distance - 1, half, 2 * distance)
        pairs = [
            (a, b) for first in firsts for a, b in zip(at(first), at(first + distance), strict=True)
        ]
        first_v = lax.ppermute(new_v, "slab", pairs)
        if level == levels - 1:
            new_v, level_v, level_b = call(
                level_kernel, [tall, square, thin], [square], new_v, new_u, cross, first_v
            )
            stored.append((distance, pairs, (level_v, level_b)))
        else:
            first_u = lax.ppermute(new_u, "slab", pairs)
            first_cross = lax.ppermute(cross, "slab", pairs)
            new_v, new_u, cross, level_v, level_b, level_u = call(
                wide_level_kernel,
                [tall, tall, square, square, thin, square],
                [square],
                new_v, new_u, cross, first_v, first_u, first_cross,
            )
            stored.append((distance, pairs, (level_v, level_b, level_u)))
    other = lax.ppermute(new_v, "slab", [(half - 1, half), (half, half - 1)])
    (value_v,) = call(center_kernel, [thin], [square, full], new_v, other, center)
    value_u = jnp.zeros_like(value_v)
    for distance, pairs, kept in reversed(stored):
        if len(kept) == 2:
            (middle,) = call(narrow_back_kernel, [thin], [], value_v, *kept)
        else:
            (middle,) = call(back_kernel, [thin], [], value_v, value_u, *kept)
        sent = lax.ppermute(
            jnp.concatenate([middle, value_u]), "slab", [(b, a) for a, b in pairs]
        )
        is_first = place % (2 * distance) == distance - 1
        value_v = jnp.where(is_first, sent[:rhs], value_v)
        value_u = jnp.where(is_first, sent[rhs:], middle)
    (result,) = call(
        final_kernel, [sources.shape], [], value_v, value_u, kept_v, kept_b, kept_u
    )
    return result


def solution(mesh):
    placed = (
        P(("energy", "slab"), "orb", None),
        P(("energy", "slab"), None, None),
        P(("energy", "slab"), ("orb", "rhs"), None),
    )
    return jax.shard_map(
        local,
        mesh=mesh,
        in_specs=placed,
        out_specs=P(("energy", "slab"), ("orb", "rhs"), None),
        check_vma=False,
    )
```

```python
import jax
import jax.numpy as jnp
from jax import lax
from jax.sharding import PartitionSpec as P
from jax.experimental import pallas as pl
from jax.experimental.pallas import tpu as pltpu

HALF = 64
LANES = 2 * HALF


def dot(left, right, dims=((1,), (0,))):
    return lax.dot_general(
        left,
        right,
        (dims, ((), ())),
        precision=lax.Precision.HIGHEST,
        preferred_element_type=jnp.float32,
    )


def dot_flipped(left, right):
    return dot(left, right, ((1,), (1,)))


def lane_sign(shape):
    lane = lax.broadcasted_iota(jnp.int32, shape, 1)
    return jnp.where(lane % LANES < HALF, -1.0, 1.0).astype(jnp.float32)


def times_i(rows):
    pieces = [
        pltpu.roll(rows[:, start : start + LANES], HALF, 1)
        for start in range(0, rows.shape[1], LANES)
    ]
    turned = pieces[0] if len(pieces) == 1 else jnp.concatenate(pieces, axis=1)
    return turned * lane_sign(turned.shape)


def interleave(rows):
    count = rows.shape[1] // LANES
    pieces = []
    for chunk in range(count):
        pieces.append(rows[:, chunk * HALF : (chunk + 1) * HALF])
        pieces.append(rows[:, (count + chunk) * HALF : (count + chunk + 1) * HALF])
    return jnp.concatenate(pieces, axis=1)


def separate(rows):
    count = rows.shape[1] // LANES
    pieces = [rows[:, 2 * chunk * HALF : (2 * chunk + 1) * HALF] for chunk in range(count)]
    pieces += [rows[:, (2 * chunk + 1) * HALF : (2 * chunk + 2) * HALF] for chunk in range(count)]
    return jnp.concatenate(pieces, axis=1)


def embed(rows):
    turned = times_i(rows)
    pieces = []
    for start in range(0, rows.shape[0], HALF):
        pieces += [rows[start : start + HALF], turned[start : start + HALF]]
    return jnp.concatenate(pieces, axis=0)


def compact(embedded):
    return jnp.concatenate(
        [embedded[start : start + HALF] for start in range(0, embedded.shape[0], LANES)], axis=0
    )


GROUP = 16
TALL = 8


def product(left, right):
    return (left[0] * right[0] - left[1] * right[1], left[0] * right[1] + left[1] * right[0])


def conjugate(value):
    return (value[0], -value[1])


def plus(left, right):
    return (left[0] + right[0], left[1] + right[1])


def minus(left, right):
    return (left[0] - right[0], left[1] - right[1])


def squared(value):
    return value[0] * value[0] + value[1] * value[1]


def scaled_by(value, factor):
    return (value[0] * factor, value[1] * factor)


def invert_pair(head, cross, tail):
    scale = 1.0 / (head * tail - squared(cross))
    return tail * scale, scaled_by(cross, -scale), head * scale


def invert_four(at):
    head = invert_pair(at[0][0][0], at[0][1], at[1][1][0])
    upper = [[at[0][2], at[0][3]], [at[1][2], at[1][3]]]
    mixed = [
        [plus(scaled_by(upper[0][j], head[0]), product(head[1], upper[1][j])) for j in range(2)],
        [
            plus(product(conjugate(head[1]), upper[0][j]), scaled_by(upper[1][j], head[2]))
            for j in range(2)
        ],
    ]

    def schur(i, j):
        return plus(
            product(conjugate(upper[0][i]), mixed[0][j]),
            product(conjugate(upper[1][i]), mixed[1][j]),
        )

    tail = invert_pair(
        at[2][2][0] - schur(0, 0)[0],
        minus(at[2][3], schur(0, 1)),
        at[3][3][0] - schur(1, 1)[0],
    )
    carried = [
        [
            plus(scaled_by(mixed[i][0], tail[0]), product(mixed[i][1], conjugate(tail[1]))),
            plus(product(mixed[i][0], tail[1]), scaled_by(mixed[i][1], tail[2])),
        ]
        for i in range(2)
    ]

    def corner(i, j):
        return plus(
            product(carried[i][0], conjugate(mixed[j][0])),
            product(carried[i][1], conjugate(mixed[j][1])),
        )

    zero = jnp.zeros_like(head[0])
    result = [[None] * 4 for _ in range(4)]
    result[0][0] = (head[0] + corner(0, 0)[0], zero)
    result[0][1] = plus(head[1], corner(0, 1))
    result[1][1] = (head[2] + corner(1, 1)[0], zero)
    result[2][2], result[2][3], result[3][3] = (tail[0], zero), tail[1], (tail[2], zero)
    for i in range(2):
        for j in range(2):
            result[i][2 + j] = (-carried[i][j][0], -carried[i][j][1])
    for i in range(4):
        for j in range(i):
            result[i][j] = conjugate(result[j][i])
    return result


def spread_row(rows, at):
    return jnp.broadcast_to(rows[at : at + 1], (TALL, LANES))


def spread_lane(rows, at):
    return jnp.broadcast_to(rows[:, at : at + 1], (TALL, LANES))


def invert_group(rows, first, sign, lane, row_id):
    parts = [rows[start : start + TALL] for start in range(0, GROUP, TALL)]
    for offset in range(0, GROUP, 4):
        step = first + offset
        home, inner = divmod(offset, TALL)
        columns = [
            [(spread_lane(part, step + at), spread_lane(part, step + at + HALF)) for at in range(4)]
            for part in parts
        ]
        inverse = invert_four(
            [
                [
                    tuple(spread_row(value, inner + i) for value in columns[home][j])
                    if j >= i
                    else None
                    for j in range(4)
                ]
                for i in range(4)
            ]
        )
        inside = (lane % HALF >= step) & (lane % HALF < step + 4)
        cleared = jnp.where(inside, 0.0, parts[home])
        turned = pltpu.roll(cleared, HALF, 1) * sign
        plain, spun = [], []
        for at in range(4):
            plain.append(spread_row(cleared, inner + at) + jnp.where(lane == step + at, 1.0, 0.0))
            spun.append(
                spread_row(turned, inner + at) + jnp.where(lane == step + at + HALF, 1.0, 0.0)
            )
        new_rows, new_spins = [], []
        for i in range(4):
            new = spin = None
            for j in range(4):
                real, imag = inverse[i][j]
                if i == j:
                    term, turn = real * plain[j], real * spun[j]
                else:
                    term = real * plain[j] + imag * spun[j]
                    turn = real * spun[j] - imag * plain[j]
                new, spin = (term, turn) if new is None else (new + term, spin + turn)
            new_rows.append(new)
            new_spins.append(spin)
        updated = []
        for index, part in enumerate(parts):
            fresh = jnp.where(inside, 0.0, part)
            for i in range(4):
                real, imag = columns[index][i]
                fresh = fresh - (real * new_rows[i] + imag * new_spins[i])
            if index == home:
                for i in range(4):
                    fresh = jnp.where(row_id == inner + i, new_rows[i], fresh)
            updated.append(fresh)
        parts = updated
    return jnp.concatenate(parts, axis=0) if len(parts) > 1 else parts[0]


def spread_out(done, spun, first):
    last = HALF - first - GROUP
    before = [jnp.zeros((first, LANES), jnp.float32)] if first else []
    after = [jnp.zeros((last, LANES), jnp.float32)] if last else []
    return jnp.concatenate(before + [done] + after + before + [spun] + after, axis=0)


def invert_small(block):
    lane = lax.broadcasted_iota(jnp.int32, (1, LANES), 1)
    row_id = lax.broadcasted_iota(jnp.int32, (TALL, 1), 0)
    sign = lane_sign((1, LANES))
    group = block[:GROUP]
    for first in range(0, HALF, GROUP):
        done = invert_group(group, first, sign, lane, row_id)
        spun = pltpu.roll(done, HALF, 1) * sign
        inside = (lane % HALF >= first) & (lane % HALF < first + GROUP)
        following = first + GROUP
        if following < HALF:
            old = block[following : following + GROUP]
            group = jnp.where(inside, 0.0, old)
            for at in range(GROUP):
                group = group - (
                    old[:, first + at : first + at + 1] * done[at : at + 1]
                    + old[:, first + at + HALF : first + at + HALF + 1] * spun[at : at + 1]
                )
        rest = jnp.where(inside, 0.0, block) - dot(
            jnp.where(inside, block, 0.0), spread_out(done, spun, first)
        )
        above = [rest[:first]] if first else []
        below = [rest[following:]] if following < HALF else []
        block = jnp.concatenate(above + [done] + below, axis=0)
    return block


def invert(ref):
    order = ref.shape[0]

    def step(k, carry):
        rows = pl.ds(pl.multiple_of(k * HALF, HALF), HALF)
        lanes = pl.ds(pl.multiple_of(k * LANES, LANES), LANES)
        small = invert_small(ref[rows, lanes])
        panel = ref[rows, :]
        ref[rows, :] = dot(small, jnp.concatenate([panel, times_i(panel)], axis=0))
        ref[rows, lanes] = small
        fresh = ref[rows, :]
        column = ref[:, lanes]
        ref[:, lanes] = jnp.zeros((order, LANES), jnp.float32)
        ref[...] = ref[...] - dot(column, jnp.concatenate([fresh, times_i(fresh)], axis=0))
        ref[rows, :] = fresh
        return carry

    lax.fori_loop(0, order // HALF, step, 0)


def eliminate(pivot_ref, to_pivot_v, to_pivot_u, block_v, block_u, load_i, load_v, load_u):
    invert(pivot_ref)
    return apply_pivot(
        pivot_ref, to_pivot_v, to_pivot_u, block_v, block_u, load_i, load_v, load_u
    )


def apply_pivot(pivot_ref, to_pivot_v, to_pivot_u, block_v, block_u, load_i, load_v, load_u):
    order, rhs = block_v.shape[0], load_i.shape[0]
    inverse = embed(pivot_ref[...])
    stacked = [compact(to_pivot_v), load_i]
    if to_pivot_u is not None:
        stacked.append(compact(to_pivot_u))
    through = dot(jnp.concatenate(stacked, axis=0), inverse)
    toward_v = dot_flipped(through[: order + rhs], to_pivot_v)
    new_v = jnp.concatenate([block_v, load_v], axis=0) - toward_v
    kept = (through[:order], through[order : order + rhs])
    if to_pivot_u is None:
        return new_v, kept
    toward_u = dot_flipped(through, to_pivot_u)
    new_u = jnp.concatenate([block_u, load_u], axis=0) - jnp.concatenate(
        [toward_u[order + rhs :], toward_u[order : order + rhs]], axis=0
    )
    return new_v, new_u, -toward_u[:order], kept + (through[order + rhs :],)


def flip_where(flip, ref, embedded):
    @pl.when(flip)
    def _():
        ref[...] = embedded.T

    @pl.when(jnp.logical_not(flip))
    def _():
        ref[...] = embedded


def is_left():
    return lax.axis_index("slab") < lax.axis_size("slab") // 2


def invert_kernel(block, inverse):
    inverse[...] = interleave(block[...])
    invert(inverse)


def interior_kernel(
    inverse, boundary, inner, outer, loads,
    new_v, new_u, cross, kept_v, kept_b, kept_u, to_v, to_u,
):
    left = is_left()
    at_interior = jnp.where(left, 0, 1)
    flip_where(left, to_v, embed(interleave(inner[...])))
    flip_where(jnp.logical_not(left), to_u, embed(interleave(outer[...])))
    load_i = interleave(loads[at_interior])
    load_v = interleave(loads[1 - at_interior])
    block_v = interleave(boundary[...])
    zero = jnp.zeros_like(block_v)
    new_v[...], new_u[...], cross[...], kept = apply_pivot(
        inverse, to_v[...], to_u[...], block_v, zero, load_i, load_v, jnp.zeros_like(load_v)
    )
    kept_v[...], kept_b[...], kept_u[...] = kept


def level_kernel(own_v, own_u, own_cross, first_v, new_v, kept_v, kept_b, pivot):
    order = pivot.shape[0]
    joined = first_v[...] + own_u[...]
    pivot[...] = joined[:order]
    new_v[...], kept = eliminate(
        pivot, embed(own_cross[...]), None, own_v[:order], None, joined[order:], own_v[order:], None
    )
    kept_v[...], kept_b[...] = kept


def wide_level_kernel(
    own_v, own_u, own_cross, first_v, first_u, first_cross,
    new_v, new_u, cross, kept_v, kept_b, kept_u, pivot,
):
    order = pivot.shape[0]
    joined = first_v[...] + own_u[...]
    pivot[...] = joined[:order]
    new_v[...], new_u[...], cross[...], kept = eliminate(
        pivot,
        embed(own_cross[...]),
        embed(first_cross[...]).T,
        own_v[:order],
        first_u[:order],
        joined[order:],
        own_v[order:],
        first_u[order:],
    )
    kept_v[...], kept_b[...], kept_u[...] = kept


def center_kernel(own, other, coupling, value, pivot, to_other):
    order = pivot.shape[0]
    flip_where(jnp.logical_not(is_left()), to_other, embed(interleave(coupling[...])))
    pivot[...] = other[:order]
    reduced, _ = eliminate(
        pivot, to_other[...], None, own[:order], None, other[order:], own[order:], None
    )
    pivot[...] = reduced[:order]
    invert(pivot)
    value[...] = dot(reduced[order:], embed(pivot[...]))


def back_kernel(value_v, value_u, kept_v, kept_b, kept_u, middle):
    middle[...] = (
        kept_b[...]
        - dot(value_v[...], embed(kept_v[...]))
        - dot(value_u[...], embed(kept_u[...]))
    )


def narrow_back_kernel(value_v, kept_v, kept_b, middle):
    middle[...] = kept_b[...] - dot(value_v[...], embed(kept_v[...]))


def final_kernel(value_v, value_u, kept_v, kept_b, kept_u, result):
    middle = (
        kept_b[...]
        - dot(value_v[...], embed(kept_v[...]))
        - dot(value_u[...], embed(kept_u[...]))
    )
    at_interior = jnp.where(is_left(), 0, 1)
    result[at_interior] = separate(middle)
    result[1 - at_interior] = separate(value_v[...])


def call(kernel, outs, scratch, *operands, flops=0):
    return pl.pallas_call(
        kernel,
        out_shape=[jax.ShapeDtypeStruct(shape, jnp.float32) for shape in outs],
        scratch_shapes=[pltpu.VMEM(shape, jnp.float32) for shape in scratch],
        cost_estimate=pl.CostEstimate(flops=flops, bytes_accessed=flops // 64, transcendentals=0)
        if flops
        else None,
        compiler_params=pltpu.CompilerParams(vmem_limit_bytes=48 * 1024 * 1024),
    )(*operands)


def gather_columns(shard):
    size = lax.axis_size("orb")
    index = lax.axis_index("orb")
    distance = 1
    while distance < size:
        theirs = lax.ppermute(shard, "orb", [(i, i ^ distance) for i in range(size)])
        first = index // distance % 2 == 0
        shard = jnp.where(
            first,
            jnp.concatenate([shard, theirs], axis=0),
            jnp.concatenate([theirs, shard], axis=0),
        )
        distance *= 2
    return shard


def local(diag_blocks, couplings, sources):
    order, width = couplings.shape[1:]
    rhs = sources.shape[1]
    slabs = lax.axis_size("slab")
    half = slabs // 2
    slab = lax.axis_index("slab")
    left = slab < half
    place = jnp.where(left, slab, slabs - 1 - slab)

    def at(position):
        return (position, slabs - 1 - position)

    shifted = lax.ppermute(couplings[0], "slab", [(i, i - 1) for i in range(half, slabs)])
    interior = gather_columns(jnp.where(left, diag_blocks[0], diag_blocks[1]))
    held = jnp.where(left, diag_blocks[1], diag_blocks[0])
    interior, held = lax.optimization_barrier((interior, held))
    boundary = gather_columns(held)
    outer = jnp.where(left, jnp.where(slab > 0, couplings[0], 0.0), shifted)
    center = jnp.where(left, shifted, couplings[0])
    square, tall, thin, full = (order, width), (order + rhs, width), (rhs, width), (width, width)

    (inverse,) = call(invert_kernel, [square], [], interior, flops=64 * order * width * width)
    new_v, new_u, cross, kept_v, kept_b, kept_u = call(
        interior_kernel,
        [tall, tall, square, square, thin, square],
        [full, full],
        inverse, boundary, couplings[1], outer, sources,
    )
    levels = half.bit_length() - 1
    stored = []
    for level in range(levels):
        distance = 2**level
        firsts = range(distance - 1, half, 2 * distance)
        pairs = [
            (a, b) for first in firsts for a, b in zip(at(first), at(first + distance), strict=True)
        ]
        first_v = lax.ppermute(new_v, "slab", pairs)
        if level == levels - 1:
            new_v, level_v, level_b = call(
                level_kernel, [tall, square, thin], [square], new_v, new_u, cross, first_v
            )
            stored.append((distance, pairs, (level_v, level_b)))
        else:
            first_u = lax.ppermute(new_u, "slab", pairs)
            first_cross = lax.ppermute(cross, "slab", pairs)
            new_v, new_u, cross, level_v, level_b, level_u = call(
                wide_level_kernel,
                [tall, tall, square, square, thin, square],
                [square],
                new_v, new_u, cross, first_v, first_u, first_cross,
            )
            stored.append((distance, pairs, (level_v, level_b, level_u)))
    other = lax.ppermute(new_v, "slab", [(half - 1, half), (half, half - 1)])
    (value_v,) = call(center_kernel, [thin], [square, full], new_v, other, center)
    value_u = jnp.zeros_like(value_v)
    for distance, pairs, kept in reversed(stored):
        if len(kept) == 2:
            (middle,) = call(narrow_back_kernel, [thin], [], value_v, *kept)
        else:
            (middle,) = call(back_kernel, [thin], [], value_v, value_u, *kept)
        sent = lax.ppermute(
            jnp.concatenate([middle, value_u]), "slab", [(b, a) for a, b in pairs]
        )
        is_first = place % (2 * distance) == distance - 1
        value_v = jnp.where(is_first, sent[:rhs], value_v)
        value_u = jnp.where(is_first, sent[rhs:], middle)
    (result,) = call(
        final_kernel, [sources.shape], [], value_v, value_u, kept_v, kept_b, kept_u
    )
    return result


def solution(mesh):
    placed = (
        P(("energy", "slab"), "orb", None),
        P(("energy", "slab"), None, None),
        P(("energy", "slab"), ("orb", "rhs"), None),
    )
    return jax.shard_map(
        local,
        mesh=mesh,
        in_specs=placed,
        out_specs=P(("energy", "slab"), ("orb", "rhs"), None),
        check_vma=False,
    )
```
